128 devices in a mesh: ex: 16 (over z, y), ey: 8 (over x, core).
Axes of the slice: x: 4, y: 4, z: 4, core: 2. Of those that a mesh axis runs over, the one named last changes fastest.
Arguments:
- tokens: bfloat16 [32768, 768], P(('ex', 'ey')), may hold values from -6 to 6
- routes: int32 [32768, 1], P(('ex', 'ey')), may hold values from 0 to 127; in each aligned block of 256 rows (0 to 255, 256 to 511, ...) at most 4 rows name the same one
- sub_expert: int32 [32768], P(('ex', 'ey')), may hold values from 0 to 1
- probability: float32 [32768], P(('ex', 'ey')), may hold values from 0.2 to 1
- weight_in: bfloat16 [256, 768, 3072], P(('ex', 'ey')), may hold values from -0.21875 to 0.21875
- weight_out: bfloat16 [256, 3072, 768], P(('ex', 'ey')), may hold values from -0.109375 to 0.109375
Outputs:
- mixed: bfloat16 [32768, 768], P(('ex', 'ey'))
The draws below stay inside these ranges and needn't reach their ends.
Inputs may be any that keep to these rules, and one draw needn't show every extreme that they name: `routes`: among the 256 tokens of one device (aligned blocks of rows), no value is named by more than 4 tokens, a bound that some block reaches.
All inputs are finite; a program needn't handle non-finite values.
Results may differ from the reference program's by a relative error of at most 0.0058.
Values may be sent and summed in bfloat16 or wider, within the bound.
A program may use at most 64 MiB of HBM per device.

```python
import math
import jax
import jax.numpy as jnp
import numpy as np
from jax import lax

D = 768
FF = 3072
EXP_DEV = 2
EXPERTS = 256
TOK_DEV = 256
TOKENS = 32768
CAP = 4
N_EX = 16
N_EY = 8


def touch_ends(entries, rng, least, high):
    index_at = [jax.random.randint(jax.random.fold_in(rng, axis), (), 0, length) for axis, length in enumerate(entries.shape)]
    main_axis = entries.shape.index(max(entries.shape))
    beside = index_at[:main_axis] + [(index_at[main_axis] + 1) % entries.shape[main_axis]] + index_at[main_axis + 1:]
    return entries.at[tuple(index_at)].set(least).at[tuple(beside)].set(high)


def block_levels(stream_key, dims, split, smallest, largest):
    loudness, own = 1.0, jax.random.fold_in(stream_key, 6)
    for position, parts in split:
        steps = jnp.exp(jax.random.uniform(jax.random.fold_in(own, position), (parts,), jnp.float32, smallest / len(split), largest / len(split)))
        loudness = loudness * jnp.repeat(steps, dims[position] // parts).reshape([-1 if axis == position else 1 for axis in range(len(dims))])
    return loudness


def shared_out(own_key, own, number, rows, number_of, top, bound, lean):
    sequence = jax.random.permutation(own_key, number_of)
    packed, common = load_shares(number_of, rows * top, bound, lean, True), load_shares(number_of, rows * top, bound, lean, False)
    places = jnp.arange(number_of)

    def named(lengths, turn):
        used = int((lengths > 0).sum())
        fixed = max(1, used // 4)
        shifted = fixed + (places - fixed + turn * (used - fixed)) % max(1, number_of - fixed)
        return jnp.zeros((number_of,), jnp.int32).at[sequence[jnp.where(places < fixed, places, shifted)]].set(jnp.asarray(lengths, jnp.int32))

    lengths = jnp.where(number % 4 == 0, named(packed, number // 4), named(common, number - number // 4 - 1))
    mixed = jax.random.permutation(jax.random.fold_in(own, 3), number_of)
    giver, sink = mixed[0:number_of // 2 * 2:2], mixed[1:number_of // 2 * 2:2]
    slack = jnp.minimum(lengths[giver] - 1, bound - lengths[sink]) // 2
    slack = jnp.where((giver == sequence[0]) | (sink == sequence[0]) | (lengths[sink] == 0), 0, jnp.maximum(slack, 0))
    shifted = jax.random.randint(jax.random.fold_in(own, 4), (number_of // 2,), 0, 1 << 20) % (slack + 1)
    lengths = lengths.at[giver].add(-shifted).at[sink].add(shifted)
    items = jnp.searchsorted(jnp.cumsum(lengths), jnp.arange(rows * top), side="right").astype(jnp.int32)
    listing = items.reshape(top, rows).T
    listing = listing[jax.random.permutation(jax.random.fold_in(own, 1), rows)]
    turn = jax.random.randint(jax.random.fold_in(own, 2), (rows, 1), 0, top)
    return jnp.take_along_axis(listing, (jnp.arange(top)[None, :] + turn) % top, axis=1)


def load_shares(count, total, bound, slope, full):
    loads = [(1 << 20) // math.isqrt(rank ** slope) + 1 for rank in range(1, count + 1)]
    largest = bound if full else min(bound, max(-(-total // count), total * loads[0] // sum(loads)))
    least = 1 if total - largest >= count - 1 else 0
    holding, spare = [largest] + [least] * (count - 1), total - largest - least * (count - 1)
    while spare > 0:
        movable = [i for i in range(1, count) if holding[i] < largest] or [i for i in range(1, count) if holding[i] < bound]
        pool, left = sum([loads[i] for i in movable]), spare
        for i in movable:
            addition = min(bound - holding[i], max(1, left * loads[i] // pool), spare)
            holding[i] = holding[i] + addition
            spare = spare - addition
    return np.array(holding)


def noise(key, dims, scale, bound, pieces=(), held_as=jnp.bfloat16):
    values = jax.random.normal(key, dims, jnp.float32) * scale
    if len(pieces) > 0:
        values = block_levels(key, dims, pieces, -0.22, 0.18) * values
    return jnp.clip(values, min=-bound, max=bound).astype(held_as)


def setup_inputs(seed: int = 0) -> dict:
    seeds = jax.random.split(jax.random.key(seed), 7)
    tokens = noise(seeds[0], (TOKENS, D), 1.0, 6.0, ((0, 128),))
    routes_keys = jax.random.split(jax.random.fold_in(seeds[1], 1), TOKENS // TOK_DEV)
    routes_turns = jax.random.permutation(jax.random.fold_in(seeds[1], 3), TOKENS // TOK_DEV)
    routes = jax.vmap(lambda own, number: shared_out(jax.random.fold_in(seeds[1], 2), own, number, TOK_DEV, N_EX * N_EY, 1, CAP, 1))(routes_keys, routes_turns).reshape((TOKENS, 1))
    sub_expert = touch_ends(jax.random.randint(seeds[2], (TOKENS,), 0, EXP_DEV), jax.random.fold_in(seeds[2], 1), 0, EXP_DEV - 1).astype(jnp.int32)
    probability = jnp.clip(0.2 + 0.8 * jax.random.uniform(seeds[3], (TOKENS,), jnp.float32) ** block_levels(seeds[3], (TOKENS,), ((0, 128),), -0.2, 0.2), 0.2, 1.0)
    weight_in = noise(seeds[4], (EXPERTS, D, FF), D ** -0.5, 0.21875, ((0, 128),))
    weight_out = noise(seeds[5], (EXPERTS, FF, D), FF ** -0.5, 0.109375, ((0, 128),))
    return {"tokens": tokens, "routes": routes, "sub_expert": sub_expert, "probability": probability, "weight_in": weight_in, "weight_out": weight_out}


def reference(tokens, routes, sub_expert, probability, weight_in, weight_out):
    route = (routes[:, 0] * EXP_DEV + sub_expert).astype(jnp.int32)
    total = tokens.shape[0]
    width = CAP * N_EX * N_EY
    order = jnp.argsort(route, stable=True).astype(jnp.int32)
    counts = jnp.zeros((EXPERTS,), jnp.int32).at[route].add(1)
    starts = (jnp.cumsum(counts) - counts).astype(jnp.int32)
    padded_order = jnp.concatenate([order, jnp.full((width,), total, jnp.int32)])
    padded_tokens = jnp.concatenate([tokens, jnp.zeros((1, tokens.shape[1]), tokens.dtype)])

    def one_expert(carry, expert):
        picks = lax.dynamic_slice_in_dim(padded_order, starts[expert], width)
        live = jnp.arange(width, dtype=jnp.int32) < counts[expert]
        picks = jnp.where(live, picks, total).astype(jnp.int32)
        rows = padded_tokens[picks]
        hidden = jax.nn.relu(jnp.dot(rows, weight_in[expert], preferred_element_type=jnp.float32)).astype(jnp.bfloat16)
        result = jnp.dot(hidden, weight_out[expert], preferred_element_type=jnp.float32).astype(jnp.bfloat16)
        carry = carry.at[picks].set(result, mode="drop")
        return carry, None

    outputs, _ = lax.scan(one_expert, jnp.zeros((total, D), jnp.bfloat16), jnp.arange(EXPERTS, dtype=jnp.int32))
    return (outputs.astype(jnp.float32) * probability[:, None]).astype(jnp.bfloat16)
```

```python
import jax
import jax.numpy as jnp
from jax import lax
from jax.experimental import pallas as pl
from jax.experimental.pallas import tpu as pltpu
from jax.sharding import PartitionSpec as P

MESH = pl.DeviceIdType.MESH
NZ, NY, NX, NC = 4, 4, 4, 2
CAP = 4
CHUNKS = 4
PER = NY * NX * NC
BF, F32 = jnp.bfloat16, jnp.float32


def position():
    e, q = lax.axis_index("ex"), lax.axis_index("ey")
    return lax.div(e, NY), lax.rem(e, NY), lax.div(q, NC), lax.rem(q, NC)


def peers(chunk, sign, visit):
    z, y, x, c = position()

    def rows(dy, carry):
        yy = lax.rem(y + NY + sign * dy, NY)
        for dx in range(NX):
            dz = lax.rem(chunk + 2 * NZ - dy - dx, NZ)
            zz = lax.rem(z + NZ + sign * dz, NZ)
            xx = lax.rem(x + NX + sign * dx, NX)
            for dc in range(NC):
                cc = lax.rem(c + dc, NC)
                visit(dy * (NX * NC) + dx * NC + dc, (zz * NY + yy, xx * NC + cc))
        return carry

    lax.fori_loop(0, NY, rows, 0)


def every(visit):
    def chunk(k, carry):
        def one(j, device):
            n = k * PER + j

            @pl.when(n != 0)
            def _():
                visit(n, device)

        peers(k, 1, one)
        return carry

    lax.fori_loop(0, CHUNKS, chunk, 0)


def iota(shape, dim):
    return lax.broadcasted_iota(jnp.int32, shape, dim)


def onehot(mask):
    return jnp.where(mask, 1.0, 0.0).astype(BF)


def kernel(
    tokens, routes, sub, win_hbm, wout_hbm, out,
    win, wout, send, recv, back, home, labels, labels_in, hidden,
    w_sem, send_sem, recv_sem, lsend_sem, lrecv_sem, bsend_sem, home_sem,
):
    half = tokens.shape[1] // 2
    n_tok = tokens.shape[0]
    z, y, x, c = position()

    barrier = pltpu.get_barrier_semaphore()
    every(
        lambda n, device: pl.semaphore_signal(
            barrier, inc=1, device_id=device, device_id_type=MESH
        )
    )
    loads = []
    for e in range(win.shape[0]):
        loads.append(pltpu.make_async_copy(win_hbm.at[e], win.at[e], w_sem.at[2 * e]))
        loads.append(pltpu.make_async_copy(wout_hbm.at[e], wout.at[e], w_sem.at[2 * e + 1]))
    for load in loads:
        load.start()

    owner = routes[...]
    oz, oy = owner // (NY * NX * NC), (owner // (NX * NC)) % NY
    ox, oc = (owner // NC) % NX, owner % NC
    dz, dy = (oz + NZ - z) % NZ, (oy + NY - y) % NY
    dx, dc = (ox + NX - x) % NX, (oc + NC - c) % NC
    number = ((dz + dy + dx) % CHUNKS) * PER + dy * (NX * NC) + dx * NC + dc
    row, lane = iota((n_tok, n_tok), 0), iota((n_tok, n_tok), 1)
    diagonal = row == lane
    number_row = number.astype(F32)
    sub_row = sub[...].astype(F32)
    number_col = jnp.sum(jnp.where(diagonal, number_row, 0.0), axis=1, keepdims=True)
    sub_col = jnp.sum(jnp.where(diagonal, sub_row, 0.0), axis=1, keepdims=True)
    same = jnp.where(number_col == number_row, 1.0, 0.0)
    slot_row = jnp.sum(jnp.where(row < lane, same, 0.0), axis=0, keepdims=True)
    slot_col = jnp.sum(jnp.where(lane < row, same, 0.0), axis=1, keepdims=True)
    target_row = (number_row * (2 * CAP) + slot_row).astype(jnp.int32)
    target_col = (number_col * (2 * CAP) + slot_col).astype(jnp.int32)

    peer = iota((CHUNKS * PER, n_tok), 0).astype(F32)
    lanes = iota((n_tok, 128), 1).astype(F32)
    chosen = jnp.where(slot_col == lanes, sub_col, 0.0).astype(BF)
    labels[...] = (
        jnp.dot(onehot(peer == number_row), chosen, preferred_element_type=F32)
        .astype(jnp.int32)
        .reshape(labels.shape)
    )

    rows = PER * 2 * CAP
    place_row = iota((rows, n_tok), 0)
    left, right = tokens[:, :half], tokens[:, half:]

    def place(k, carry):
        at = place_row + k * rows
        block = jnp.dot(onehot(at == target_row), left, preferred_element_type=F32)
        block += jnp.dot(onehot(at == target_row + CAP), right, preferred_element_type=F32)
        send[pl.ds(k * PER, PER)] = block.astype(BF).reshape(PER, 2 * CAP, half)
        return carry

    lax.fori_loop(0, CHUNKS, place, 0)

    pl.semaphore_wait(barrier, CHUNKS * PER - 1)

    def dispatch(k, carry):
        def one(j, device):
            n = k * PER + j

            def remote():
                pltpu.make_async_remote_copy(
                    labels.at[n], labels_in.at[n], lsend_sem, lrecv_sem.at[k],
                    device_id=device, device_id_type=MESH,
                ).start()
                pltpu.make_async_remote_copy(
                    send.at[n], recv.at[n], send_sem, recv_sem.at[k],
                    device_id=device, device_id_type=MESH,
                ).start()

            pl.when(n != 0)(remote)

        peers(k, 1, one)
        return carry

    pltpu.make_async_copy(labels.at[0], labels_in.at[0], lrecv_sem.at[0]).start()
    pltpu.make_async_copy(send.at[0], recv.at[0], recv_sem.at[0]).start()
    lax.fori_loop(0, CHUNKS, dispatch, 0)

    for load in loads:
        load.wait()

    m = PER * CAP
    to, fro = iota((rows, rows), 0), iota((rows, rows), 1)

    def origin(r):
        h, p = r // m, r % m
        return (p // CAP) * (2 * CAP) + h * CAP + p % CAP

    split = onehot(fro == origin(to))
    join = onehot(to == origin(fro))
    spread = onehot(iota((m, PER), 0) // CAP == iota((m, PER), 1))
    own_lane = iota((m, 128), 0) % CAP == iota((m, 128), 1)

    def compute(k, carry):
        mine = pl.ds(k * PER, PER)
        pltpu.make_async_copy(labels.at[mine], labels_in.at[mine], lrecv_sem.at[k]).wait()
        pltpu.make_async_copy(send.at[mine], recv.at[mine], recv_sem.at[k]).wait()
        label = jnp.dot(
            spread,
            labels_in[mine].reshape(PER, 128).astype(F32).astype(BF),
            preferred_element_type=F32,
        )
        label = jnp.sum(jnp.where(own_lane, label, 0.0), axis=1, keepdims=True)
        arrived = recv[mine].reshape(rows, half)
        halves = jnp.dot(split, arrived, preferred_element_type=F32)
        batch = jnp.concatenate([halves[:m], halves[m:]], axis=1)
        total = None
        for e in range(win.shape[0]):
            part = jnp.where(label == e, batch, 0.0).astype(BF)
            hidden[...] = jnp.maximum(
                jnp.dot(part, win[e], preferred_element_type=F32), 0.0
            ).astype(BF)
            result = jnp.dot(hidden[...], wout[e], preferred_element_type=F32)
            total = result if total is None else total + result
        total = total.astype(BF)
        stacked = jnp.concatenate([total[:, :half], total[:, half:]], axis=0)
        block = jnp.dot(join, stacked, preferred_element_type=F32).astype(BF)
        back[mine] = block.reshape(PER, 2 * CAP, half)

        def one(j, device):
            n = k * PER + j

            @pl.when(n != 0)
            def _():
                pltpu.make_async_remote_copy(
                    back.at[n], home.at[n], bsend_sem, home_sem.at[k],
                    device_id=device, device_id_type=MESH,
                ).start()


        peers(k, -1, one)

        @pl.when(k == 0)
        def _():
            pltpu.make_async_copy(back.at[0], home.at[0], home_sem.at[0]).start()

        return carry

    lax.fori_loop(0, CHUNKS, compute, 0)

    take_lane = iota((n_tok, rows), 1)
    out_left = out_right = None
    for k in range(CHUNKS):
        mine = pl.ds(k * PER, PER)
        at = take_lane + k * rows
        take_left = onehot(at == target_col)
        take_right = onehot(at == target_col + CAP)
        pltpu.make_async_copy(back.at[mine], home.at[mine], home_sem.at[k]).wait()
        returned = home[mine].reshape(rows, half)
        a = jnp.dot(take_left, returned, preferred_element_type=F32)
        b = jnp.dot(take_right, returned, preferred_element_type=F32)
        out_left = a if k == 0 else out_left + a
        out_right = b if k == 0 else out_right + b
    out[:, :half] = out_left.astype(BF)
    out[:, half:] = out_right.astype(BF)

    others = pl.ds(1, CHUNKS * PER - 1)
    pltpu.make_async_copy(labels.at[others], labels_in.at[others], lsend_sem).wait()
    pltpu.make_async_copy(send.at[others], recv.at[others], send_sem).wait()
    pltpu.make_async_copy(back.at[others], home.at[others], bsend_sem).wait()


def local(tokens, routes, sub_expert, probability, weight_in, weight_out):
    n_tok, width = tokens.shape
    experts, _, units = weight_in.shape
    n = CHUNKS * PER
    vmem, hbm = pl.BlockSpec(memory_space=pltpu.VMEM), pl.BlockSpec(memory_space=pl.ANY)
    blocks = pltpu.VMEM((n, 2 * CAP, width // 2), BF)
    dma = pltpu.SemaphoreType.DMA
    gathered = pl.pallas_call(
        kernel,
        out_shape=jax.ShapeDtypeStruct((n_tok, width), BF),
        in_specs=[vmem, vmem, vmem, hbm, hbm],
        out_specs=vmem,
        scratch_shapes=[
            pltpu.VMEM(weight_in.shape, BF),
            pltpu.VMEM(weight_out.shape, BF),
            blocks, blocks, blocks, blocks,
            pltpu.VMEM((n, 1, 128), jnp.int32),
            pltpu.VMEM((n, 1, 128), jnp.int32),
            pltpu.VMEM((PER * CAP, units), BF),
            dma((2 * experts,)), dma, dma((CHUNKS,)), dma, dma((CHUNKS,)), dma, dma((CHUNKS,)),
        ],
        compiler_params=pltpu.CompilerParams(
            collective_id=0, has_side_effects=True, vmem_limit_bytes=48 << 20
        ),
    )(tokens, routes.reshape(1, n_tok), sub_expert.reshape(1, n_tok), weight_in, weight_out)
    return (gathered.astype(F32) * probability[:, None]).astype(BF)


def solution(mesh):
    return jax.shard_map(
        local,
        mesh=mesh,
        in_specs=(
            P(("ex", "ey"), None),
            P(("ex", "ey"), None),
            P(("ex", "ey")),
            P(("ex", "ey")),
            P(("ex", "ey"), None, None),
            P(("ex", "ey"), None, None),
        ),
        out_specs=P(("ex", "ey"), None),
        check_vma=False,
    )
```

```python
import jax
import jax.numpy as jnp
from jax import lax
from jax.experimental import pallas as pl
from jax.experimental.pallas import tpu as pltpu
from jax.sharding import PartitionSpec as P

MESH = pl.DeviceIdType.MESH
NZ, NY, NX, NC = 4, 4, 4, 2
CAP = 4
CHUNKS = 4
PER = NZ * NY * NX * NC // CHUNKS
BF, F32 = jnp.bfloat16, jnp.float32


def chip_order():
    chips = [(a, b, c) for a in range(NZ) for b in range(NY) for c in range(NX)]

    def kind(o):
        return "".join(str(d) for d in sorted((min(d, 4 - d) for d in o), reverse=True))

    def group(name, parity=None):
        found = [o for o in chips if kind(o) == name]
        if parity is None:
            return found
        return [o for o in found if sum(d == 3 for d in o) % 2 == parity]

    bent = group("210")
    near = group("000") + group("100") + group("200") + group("110", 0)
    second = group("110", 1) + group("111") + [bent[0], bent[-1]]
    middle = bent[1:-1] + group("211", 0)
    far = group("211", 1) + group("220") + group("221") + group("222")
    return near + middle + far + second


ORDER = chip_order()
SIDE = len(ORDER) // CHUNKS


def position():
    e, q = lax.axis_index("ex"), lax.axis_index("ey")
    return lax.div(e, NY), lax.rem(e, NY), lax.div(q, NC), lax.rem(q, NC)


def peers(chunk, sign, visit):
    z, y, x, c = position()
    flags = [jnp.where(chunk == k, 1, 0) for k in range(1, CHUNKS)]

    def offset(i, axis):
        values = [ORDER[k * SIDE + i][axis] for k in range(CHUNKS)]
        total = values[0]
        for flag, value in zip(flags, values[1:]):
            if value != values[0]:
                total = total + flag * (value - values[0])
        return total

    for i in reversed(range(SIDE)):
        dz, dy, dx = (offset(i, axis) for axis in range(3))
        zz = lax.rem(z + NZ + sign * dz, NZ)
        yy = lax.rem(y + NY + sign * dy, NY)
        xx = lax.rem(x + NX + sign * dx, NX)
        for dc in reversed(range(NC)):
            device = (zz * NY + yy, xx * NC + lax.rem(c + dc, NC))
            n = chunk * PER + i * NC + dc
            if i + dc == 0:
                pl.when(n != 0)(lambda n=n, device=device: visit(n, device))
            else:
                visit(n, device)


def iota(shape, dim):
    return lax.broadcasted_iota(jnp.int32, shape, dim)


def onehot(mask):
    return jnp.where(mask, 1.0, 0.0).astype(BF)


def push(src, dst, send_sem, recv_sem, device):
    pltpu.make_async_remote_copy(
        src, dst, send_sem, recv_sem, device_id=device, device_id_type=MESH
    ).start()


def kernel(
    tokens_hbm, routes_hbm, sub_hbm, win_hbm, wout_hbm, out,
    tokens, routes, sub, win, wout, send, recv, back, home, labels, labels_in, hidden,
    in_sem, w_sem, send_sem, recv_sem, lsend_sem, lrecv_sem, bsend_sem, home_sem,
):
    n_tok, half = tokens.shape[0], tokens.shape[1] // 2
    z, y, x, c = position()

    barrier = pltpu.get_barrier_semaphore()

    def greet(i, carry):
        peers(
            lax.rem(CHUNKS + 2 - i, CHUNKS),
            1,
            lambda n, device: pl.semaphore_signal(
                barrier, inc=1, device_id=device, device_id_type=MESH
            ),
        )
        return carry

    lax.fori_loop(0, CHUNKS, greet, 0)
    small = [
        pltpu.make_async_copy(src, dst, in_sem.at[i])
        for i, (src, dst) in enumerate(
            ((routes_hbm, routes), (sub_hbm, sub), (tokens_hbm, tokens))
        )
    ]
    loads = []
    for e in range(win.shape[0]):
        loads.append(pltpu.make_async_copy(win_hbm.at[e], win.at[e], w_sem.at[2 * e]))
        loads.append(pltpu.make_async_copy(wout_hbm.at[e], wout.at[e], w_sem.at[2 * e + 1]))
    for load in small:
        load.start()
    for load in small:
        load.wait()
    for load in loads:
        load.start()

    owner = routes[...]
    dz = ((owner >> 5) + (NZ - z)) & (NZ - 1)
    dy = ((owner >> 3) + (NY - y)) & (NY - 1)
    dx = ((owner >> 1) + (NX - x)) & (NX - 1)
    dc = (owner + (NC - c)) & (NC - 1)
    chip = dz * (NY * NX) + dy * NX + dx
    rank = jnp.zeros_like(chip)
    for i, (a, b, d) in enumerate(ORDER):
        rank = jnp.where(chip == a * (NY * NX) + b * NX + d, i, rank)
    number = rank * NC + dc
    row, lane = iota((n_tok, n_tok), 0), iota((n_tok, n_tok), 1)
    diagonal = row == lane
    number_row = number.astype(F32)
    sub_row = sub[...].astype(F32)
    number_col = jnp.sum(jnp.where(diagonal, number_row, 0.0), axis=1, keepdims=True)
    sub_col = jnp.sum(jnp.where(diagonal, sub_row, 0.0), axis=1, keepdims=True)
    same = jnp.where(number_col == number_row, 1.0, 0.0)
    slot_row = jnp.sum(jnp.where(row < lane, same, 0.0), axis=0, keepdims=True)
    slot_col = jnp.sum(jnp.where(lane < row, same, 0.0), axis=1, keepdims=True)
    target_row = (number_row * (2 * CAP) + slot_row).astype(jnp.int32)
    target_col = (number_col * (2 * CAP) + slot_col).astype(jnp.int32)

    peer = iota((CHUNKS * PER, n_tok), 0).astype(F32)
    lanes = iota((n_tok, 128), 1).astype(F32)
    chosen = jnp.where(slot_col == lanes, sub_col, 0.0).astype(BF)
    labels[...] = (
        jnp.dot(onehot(peer == number_row), chosen, preferred_element_type=F32)
        .astype(jnp.int32)
        .reshape(labels.shape)
    )

    rows = PER * 2 * CAP
    place_row = iota((rows, n_tok), 0)

    def place(k, carry):
        at = place_row + k * rows
        block = jnp.dot(
            onehot(at == target_row), tokens[:, :half], preferred_element_type=F32
        )
        block += jnp.dot(
            onehot(at == target_row + CAP), tokens[:, half:], preferred_element_type=F32
        )
        send[pl.ds(k * PER, PER)] = block.astype(BF).reshape(PER, 2 * CAP, half)
        return carry

    lax.fori_loop(0, CHUNKS, place, 0)

    pl.semaphore_wait(barrier, CHUNKS * PER - 1)

    pltpu.make_async_copy(labels.at[0], labels_in.at[0], lrecv_sem.at[0]).start()
    pltpu.make_async_copy(send.at[0], recv.at[0], recv_sem.at[0]).start()

    def dispatch(k, carry):
        def visit(n, device):
            push(labels.at[n], labels_in.at[n], lsend_sem, lrecv_sem.at[k], device)
            push(send.at[n], recv.at[n], send_sem, recv_sem.at[k], device)

        peers(k, 1, visit)
        return carry

    lax.fori_loop(0, CHUNKS, dispatch, 0)

    m = PER * CAP
    to, fro = iota((rows, rows), 0), iota((rows, rows), 1)

    def origin(r):
        return ((r & (m - 1)) >> 2) * (2 * CAP) + (r >> 7) * CAP + (r & (CAP - 1))

    split = onehot(fro == origin(to))
    join = onehot(to == origin(fro))
    spread = onehot((iota((m, PER), 0) >> 2) == iota((m, PER), 1))
    own_lane = (iota((m, 128), 0) & (CAP - 1)) == iota((m, 128), 1)

    for load in loads:
        load.wait()

    def compute(k, carry):
        mine = pl.ds(k * PER, PER)
        pltpu.make_async_copy(labels.at[mine], labels_in.at[mine], lrecv_sem.at[k]).wait()
        label = jnp.dot(
            spread,
            labels_in[mine].reshape(PER, 128).astype(F32).astype(BF),
            preferred_element_type=F32,
        )
        label = jnp.sum(jnp.where(own_lane, label, 0.0), axis=1, keepdims=True)
        pltpu.make_async_copy(send.at[mine], recv.at[mine], recv_sem.at[k]).wait()
        arrived = recv[mine].reshape(rows, half)
        halves = jnp.dot(split, arrived, preferred_element_type=F32)
        batch = jnp.concatenate([halves[:m], halves[m:]], axis=1)
        total = None
        for e in range(win.shape[0]):
            part = jnp.where(label == e, batch, 0.0).astype(BF)
            hidden[...] = jnp.maximum(
                jnp.dot(part, win[e], preferred_element_type=F32), 0.0
            ).astype(BF)
            result = jnp.dot(hidden[...], wout[e], preferred_element_type=F32)
            total = result if total is None else total + result
        total = total.astype(BF)
        stacked = jnp.concatenate([total[:, :half], total[:, half:]], axis=0)
        block = jnp.dot(join, stacked, preferred_element_type=F32).astype(BF)
        back[mine] = block.reshape(PER, 2 * CAP, half)

        @pl.when(k == 0)
        def _():
            pltpu.make_async_copy(back.at[0], home.at[0], home_sem.at[0]).start()

        peers(
            k,
            -1,
            lambda n, device: push(back.at[n], home.at[n], bsend_sem, home_sem.at[k], device),
        )
        return carry

    lax.fori_loop(0, CHUNKS, compute, 0)

    take_lane = iota((n_tok, rows), 1)
    out_left = out_right = None
    for k in range(CHUNKS):
        mine = pl.ds(k * PER, PER)
        at = take_lane + k * rows
        take_left = onehot(at == target_col)
        take_right = onehot(at == target_col + CAP)
        pltpu.make_async_copy(back.at[mine], home.at[mine], home_sem.at[k]).wait()
        returned = home[mine].reshape(rows, half)
        a = jnp.dot(take_left, returned, preferred_element_type=F32)
        b = jnp.dot(take_right, returned, preferred_element_type=F32)
        out_left = a if k == 0 else out_left + a
        out_right = b if k == 0 else out_right + b
    out[:, :half] = out_left.astype(BF)
    out[:, half:] = out_right.astype(BF)

    others = pl.ds(1, CHUNKS * PER - 1)
    pltpu.make_async_copy(labels.at[others], labels_in.at[others], lsend_sem).wait()
    pltpu.make_async_copy(send.at[others], recv.at[others], send_sem).wait()
    pltpu.make_async_copy(back.at[others], home.at[others], bsend_sem).wait()


def local(tokens, routes, sub_expert, probability, weight_in, weight_out):
    n_tok, width = tokens.shape
    experts, _, units = weight_in.shape
    n = CHUNKS * PER
    blocks = pltpu.VMEM((n, 2 * CAP, width // 2), BF)
    dma = pltpu.SemaphoreType.DMA
    gathered = pl.pallas_call(
        kernel,
        out_shape=jax.ShapeDtypeStruct((n_tok, width), BF),
        in_specs=[pl.BlockSpec(memory_space=pltpu.MemorySpace.HBM)] * 5,
        out_specs=pl.BlockSpec(memory_space=pltpu.VMEM),
        scratch_shapes=[
            pltpu.VMEM((n_tok, width), BF),
            pltpu.VMEM((1, n_tok), jnp.int32),
            pltpu.VMEM((1, n_tok), jnp.int32),
            pltpu.VMEM(weight_in.shape, BF),
            pltpu.VMEM(weight_out.shape, BF),
            blocks, blocks, blocks, blocks,
            pltpu.VMEM((n, 1, 128), jnp.int32),
            pltpu.VMEM((n, 1, 128), jnp.int32),
            pltpu.VMEM((PER * CAP, units), BF),
            dma((3,)), dma((2 * experts,)),
            dma, dma((CHUNKS,)), dma, dma((CHUNKS,)), dma, dma((CHUNKS,)),
        ],
        compiler_params=pltpu.CompilerParams(
            collective_id=0, has_side_effects=True, vmem_limit_bytes=56000000
        ),
    )(tokens, routes.reshape(1, n_tok), sub_expert.reshape(1, n_tok), weight_in, weight_out)
    return (gathered.astype(F32) * probability[:, None]).astype(BF)


def solution(mesh):
    return jax.shard_map(
        local,
        mesh=mesh,
        in_specs=(
            P(("ex", "ey"), None),
            P(("ex", "ey"), None),
            P(("ex", "ey")),
            P(("ex", "ey")),
            P(("ex", "ey"), None, None),
            P(("ex", "ey"), None, None),
        ),
        out_specs=P(("ex", "ey"), None),
        check_vma=False,
    )
```

```python
import jax
import jax.numpy as jnp
from jax import lax
from jax.experimental import pallas as pl
from jax.experimental.pallas import tpu as pltpu
from jax.sharding import PartitionSpec as P

MESH = pl.DeviceIdType.MESH
NZ, NY, NX, NC = 4, 4, 4, 2
CAP = 4
CHUNKS = 4
PER = NZ * NY * NX * NC // CHUNKS
BF, F32 = jnp.bfloat16, jnp.float32


def chip_order():
    chips = [(a, b, c) for a in range(NZ) for b in range(NY) for c in range(NX)]

    def kind(o):
        return "".join(str(d) for d in sorted((min(d, 4 - d) for d in o), reverse=True))

    def group(name, parity=None):
        found = [o for o in chips if kind(o) == name]
        if parity is None:
            return found
        return [o for o in found if sum(d == 3 for d in o) % 2 == parity]

    bent = group("210")
    near = group("000") + group("100") + group("200") + group("110", 0)
    second = group("110", 1) + group("111") + [bent[0], bent[-1]]
    middle = bent[1:-1] + group("211", 0)
    far = group("211", 1) + group("220") + group("221") + group("222")
    return near + middle + far + second


ORDER = chip_order()
SIDE = len(ORDER) // CHUNKS


def position():
    e, q = lax.axis_index("ex"), lax.axis_index("ey")
    return lax.div(e, NY), lax.rem(e, NY), lax.div(q, NC), lax.rem(q, NC)


def peers(chunk, sign, visit):
    z, y, x, c = position()
    flags = [jnp.where(chunk == k, 1, 0) for k in range(1, CHUNKS)]

    def offset(i, axis):
        values = [ORDER[k * SIDE + i][axis] for k in range(CHUNKS)]
        total = values[0]
        for flag, value in zip(flags, values[1:]):
            if value != values[0]:
                total = total + flag * (value - values[0])
        return total

    for i in reversed(range(SIDE)):
        dz, dy, dx = (offset(i, axis) for axis in range(3))
        zz = lax.rem(z + NZ + sign * dz, NZ)
        yy = lax.rem(y + NY + sign * dy, NY)
        xx = lax.rem(x + NX + sign * dx, NX)
        for dc in reversed(range(NC)):
            device = (zz * NY + yy, xx * NC + lax.rem(c + dc, NC))
            n = chunk * PER + i * NC + dc
            if i + dc == 0:
                pl.when(n != 0)(lambda n=n, device=device: visit(n, device))
            else:
                visit(n, device)


def iota(shape, dim):
    return lax.broadcasted_iota(jnp.int32, shape, dim)


def onehot(mask):
    return jnp.where(mask, 1.0, 0.0).astype(BF)


def push(src, dst, send_sem, recv_sem, device):
    pltpu.make_async_remote_copy(
        src, dst, send_sem, recv_sem, device_id=device, device_id_type=MESH
    ).start()


def kernel(
    tokens_hbm, routes_hbm, sub_hbm, win_hbm, wout_hbm, out,
    tokens, routes, sub, win, wout, send, recv, back, home, labels, labels_in, hidden,
    in_sem, w_sem, send_sem, recv_sem, lsend_sem, lrecv_sem, bsend_sem, home_sem,
):
    n_tok, half = tokens.shape[0], tokens.shape[1] // 2
    units = win.shape[2]
    z, y, x, c = position()

    barrier = pltpu.get_barrier_semaphore()

    def greet(i, carry):
        peers(
            lax.rem(CHUNKS + 2 - i, CHUNKS),
            1,
            lambda n, device: pl.semaphore_signal(
                barrier, inc=1, device_id=device, device_id_type=MESH
            ),
        )
        return carry

    lax.fori_loop(0, CHUNKS, greet, 0)
    small = [
        pltpu.make_async_copy(src, dst, in_sem.at[i])
        for i, (src, dst) in enumerate(
            ((routes_hbm, routes), (sub_hbm, sub), (tokens_hbm, tokens))
        )
    ]
    loads = []
    for e in range(win.shape[0]):
        loads.append(pltpu.make_async_copy(win_hbm.at[e], win.at[e], w_sem.at[2 * e]))
        loads.append(pltpu.make_async_copy(
            wout_hbm.at[e], wout.at[pl.ds(e * units, units)], w_sem.at[2 * e + 1]
        ))
    for load in small:
        load.start()
    for load in small:
        load.wait()
    for load in loads:
        load.start()

    owner = routes[...]
    dz = ((owner >> 5) + (NZ - z)) & (NZ - 1)
    dy = ((owner >> 3) + (NY - y)) & (NY - 1)
    dx = ((owner >> 1) + (NX - x)) & (NX - 1)
    dc = (owner + (NC - c)) & (NC - 1)
    chip = dz * (NY * NX) + dy * NX + dx
    rank = jnp.zeros_like(chip)
    for i, (a, b, d) in enumerate(ORDER):
        rank = jnp.where(chip == a * (NY * NX) + b * NX + d, i, rank)
    number = rank * NC + dc
    row, lane = iota((n_tok, n_tok), 0), iota((n_tok, n_tok), 1)
    diagonal = row == lane
    number_row = number.astype(F32)
    sub_row = sub[...].astype(F32)
    number_col = jnp.sum(jnp.where(diagonal, number_row, 0.0), axis=1, keepdims=True)
    sub_col = jnp.sum(jnp.where(diagonal, sub_row, 0.0), axis=1, keepdims=True)
    same = jnp.where(number_col == number_row, 1.0, 0.0)
    slot_row = jnp.sum(jnp.where(row < lane, same, 0.0), axis=0, keepdims=True)
    slot_col = jnp.sum(jnp.where(lane < row, same, 0.0), axis=1, keepdims=True)
    target_row = (number_row * (2 * CAP) + slot_row).astype(jnp.int32)
    target_col = (number_col * (2 * CAP) + slot_col).astype(jnp.int32)

    peer = iota((CHUNKS * PER, n_tok), 0).astype(F32)
    lanes = iota((n_tok, 128), 1).astype(F32)
    chosen = jnp.where(slot_col == lanes, sub_col, 0.0).astype(BF)
    labels[...] = (
        jnp.dot(onehot(peer == number_row), chosen, preferred_element_type=F32)
        .astype(jnp.int32)
        .reshape(labels.shape)
    )

    rows = PER * 2 * CAP
    place_row = iota((rows, n_tok), 0)

    def place(k, carry):
        at = place_row + k * rows
        block = jnp.dot(
            onehot(at == target_row), tokens[:, :half], preferred_element_type=F32
        )
        block += jnp.dot(
            onehot(at == target_row + CAP), tokens[:, half:], preferred_element_type=F32
        )
        send[pl.ds(k * PER, PER)] = block.astype(BF).reshape(PER, 2 * CAP, half)
        return carry

    lax.fori_loop(0, CHUNKS, place, 0)

    pl.semaphore_wait(barrier, CHUNKS * PER - 1)

    pltpu.make_async_copy(labels.at[0], labels_in.at[0], lrecv_sem.at[0]).start()
    pltpu.make_async_copy(send.at[0], recv.at[0], recv_sem.at[0]).start()

    def dispatch(k, carry):
        def visit(n, device):
            push(labels.at[n], labels_in.at[n], lsend_sem, lrecv_sem.at[k], device)
            push(send.at[n], recv.at[n], send_sem, recv_sem.at[k], device)

        peers(k, 1, visit)
        return carry

    lax.fori_loop(0, CHUNKS, dispatch, 0)

    m = PER * CAP
    to, fro = iota((rows, rows), 0), iota((rows, rows), 1)

    def origin(r):
        return ((r & (m - 1)) >> 2) * (2 * CAP) + (r >> 7) * CAP + (r & (CAP - 1))

    split = onehot(fro == origin(to))
    join = onehot(to == origin(fro))
    spread = onehot((iota((m, PER), 0) >> 2) == iota((m, PER), 1))
    own_lane = (iota((m, 128), 0) & (CAP - 1)) == iota((m, 128), 1)

    for load in loads:
        load.wait()

    def compute(k, carry):
        mine = pl.ds(k * PER, PER)
        pltpu.make_async_copy(labels.at[mine], labels_in.at[mine], lrecv_sem.at[k]).wait()
        label = jnp.dot(
            spread,
            labels_in[mine].reshape(PER, 128).astype(F32).astype(BF),
            preferred_element_type=F32,
        )
        label = jnp.sum(jnp.where(own_lane, label, 0.0), axis=1, keepdims=True)
        pltpu.make_async_copy(send.at[mine], recv.at[mine], recv_sem.at[k]).wait()
        arrived = recv[mine].reshape(rows, half)
        halves = jnp.dot(split, arrived, preferred_element_type=F32)
        batch = jnp.concatenate([halves[:m], halves[m:]], axis=1)
        for e in range(win.shape[0]):
            part = jnp.where(label == e, batch, 0.0).astype(BF)
            hidden[:, e * units : (e + 1) * units] = jnp.maximum(
                jnp.dot(part, win[e], preferred_element_type=F32), 0.0
            ).astype(BF)
        total = jnp.dot(hidden[...], wout[...], preferred_element_type=F32)
        total = total.astype(BF)
        stacked = jnp.concatenate([total[:, :half], total[:, half:]], axis=0)
        block = jnp.dot(join, stacked, preferred_element_type=F32).astype(BF)
        back[mine] = block.reshape(PER, 2 * CAP, half)

        @pl.when(k == 0)
        def _():
            pltpu.make_async_copy(back.at[0], home.at[0], home_sem.at[0]).start()

        peers(
            k,
            -1,
            lambda n, device: push(back.at[n], home.at[n], bsend_sem, home_sem.at[k], device),
        )
        return carry

    lax.fori_loop(0, CHUNKS, compute, 0)

    take_lane = iota((n_tok, rows), 1)
    out_left = out_right = None
    for k in (0, 1, 3, 2):
        mine = pl.ds(k * PER, PER)
        at = take_lane + k * rows
        take_left = onehot(at == target_col)
        take_right = onehot(at == target_col + CAP)
        pltpu.make_async_copy(back.at[mine], home.at[mine], home_sem.at[k]).wait()
        returned = home[mine].reshape(rows, half)
        a = jnp.dot(take_left, returned, preferred_element_type=F32)
        b = jnp.dot(take_right, returned, preferred_element_type=F32)
        out_left = a if k == 0 else out_left + a
        out_right = b if k == 0 else out_right + b
    out[:, :half] = out_left.astype(BF)
    out[:, half:] = out_right.astype(BF)

    others = pl.ds(1, CHUNKS * PER - 1)
    pltpu.make_async_copy(labels.at[others], labels_in.at[others], lsend_sem).wait()
    pltpu.make_async_copy(send.at[others], recv.at[others], send_sem).wait()
    pltpu.make_async_copy(back.at[others], home.at[others], bsend_sem).wait()


def local(tokens, routes, sub_expert, probability, weight_in, weight_out):
    n_tok, width = tokens.shape
    experts, _, units = weight_in.shape
    n = CHUNKS * PER
    blocks = pltpu.VMEM((n, 2 * CAP, width // 2), BF)
    dma = pltpu.SemaphoreType.DMA
    gathered = pl.pallas_call(
        kernel,
        out_shape=jax.ShapeDtypeStruct((n_tok, width), BF),
        in_specs=[pl.BlockSpec(memory_space=pltpu.MemorySpace.HBM)] * 5,
        out_specs=pl.BlockSpec(memory_space=pltpu.VMEM),
        scratch_shapes=[
            pltpu.VMEM((n_tok, width), BF),
            pltpu.VMEM((1, n_tok), jnp.int32),
            pltpu.VMEM((1, n_tok), jnp.int32),
            pltpu.VMEM(weight_in.shape, BF),
            pltpu.VMEM((experts * units, width), BF),
            blocks, blocks, blocks, blocks,
            pltpu.VMEM((n, 1, 128), jnp.int32),
            pltpu.VMEM((n, 1, 128), jnp.int32),
            pltpu.VMEM((PER * CAP, experts * units), BF),
            dma((3,)), dma((2 * experts,)),
            dma, dma((CHUNKS,)), dma, dma((CHUNKS,)), dma, dma((CHUNKS,)),
        ],
        compiler_params=pltpu.CompilerParams(
            collective_id=0, has_side_effects=True, vmem_limit_bytes=56000000
        ),
    )(tokens, routes.reshape(1, n_tok), sub_expert.reshape(1, n_tok), weight_in, weight_out)
    return (gathered.astype(F32) * probability[:, None]).astype(BF)


def solution(mesh):
    return jax.shard_map(
        local,
        mesh=mesh,
        in_specs=(
            P(("ex", "ey"), None),
            P(("ex", "ey"), None),
            P(("ex", "ey")),
            P(("ex", "ey")),
            P(("ex", "ey"), None, None),
            P(("ex", "ey"), None, None),
        ),
        out_specs=P(("ex", "ey"), None),
        check_vma=False,
    )
```

```python
import jax
import jax.numpy as jnp
from jax import lax
from jax.experimental import pallas as pl
from jax.experimental.pallas import tpu as pltpu
from jax.sharding import PartitionSpec as P

MESH = pl.DeviceIdType.MESH
NZ, NY, NX, NC = 4, 4, 4, 2
CAP = 4
CHUNKS = 4
PER = NZ * NY * NX * NC // CHUNKS
BF, F32 = jnp.bfloat16, jnp.float32


def chip_order():
    chips = [(a, b, c) for a in range(NZ) for b in range(NY) for c in range(NX)]

    def kind(o):
        return "".join(str(d) for d in sorted((min(d, 4 - d) for d in o), reverse=True))

    def group(name, parity=None):
        found = [o for o in chips if kind(o) == name]
        if parity is None:
            return found
        return [o for o in found if sum(d == 3 for d in o) % 2 == parity]

    bent = group("210")
    near = group("000") + group("100") + group("200") + group("110", 0)
    second = group("110", 1) + group("111") + [bent[0], bent[-1]]
    middle = bent[1:-1] + group("211", 0)
    far = group("211", 1) + group("220") + group("221") + group("222")
    return near + middle + far + second


ORDER = chip_order()
SIDE = len(ORDER) // CHUNKS


def position():
    e, q = lax.axis_index("ex"), lax.axis_index("ey")
    return lax.div(e, NY), lax.rem(e, NY), lax.div(q, NC), lax.rem(q, NC)


def peers(chunk, sign, visit):
    z, y, x, c = position()
    flags = [jnp.where(chunk == k, 1, 0) for k in range(1, CHUNKS)]

    def offset(i, axis):
        values = [ORDER[k * SIDE + i][axis] for k in range(CHUNKS)]
        total = values[0]
        for flag, value in zip(flags, values[1:]):
            if value != values[0]:
                total = total + flag * (value - values[0])
        return total

    for i in reversed(range(SIDE)):
        dz, dy, dx = (offset(i, axis) for axis in range(3))
        zz = lax.rem(z + NZ + sign * dz, NZ)
        yy = lax.rem(y + NY + sign * dy, NY)
        xx = lax.rem(x + NX + sign * dx, NX)
        for dc in reversed(range(NC)):
            device = (zz * NY + yy, xx * NC + lax.rem(c + dc, NC))
            n = chunk * PER + i * NC + dc
            if i + dc == 0:
                pl.when(n != 0)(lambda n=n, device=device: visit(n, device))
            else:
                visit(n, device)


def iota(shape, dim):
    return lax.broadcasted_iota(jnp.int32, shape, dim)


def onehot(mask):
    return jnp.where(mask, 1.0, 0.0).astype(BF)


def push(src, dst, send_sem, recv_sem, device):
    pltpu.make_async_remote_copy(
        src, dst, send_sem, recv_sem, device_id=device, device_id_type=MESH
    ).start()


def kernel(
    tokens_hbm, routes_hbm, sub_hbm, win_hbm, wout_hbm, out,
    tokens, routes, sub, win, wout, send, recv, back, home, labels, labels_in, hidden,
    in_sem, w_sem, send_sem, recv_sem, lsend_sem, lrecv_sem, bsend_sem, home_sem,
):
    n_tok, half = tokens.shape[0], tokens.shape[1] // 2
    units = win.shape[2]
    z, y, x, c = position()

    barrier = pltpu.get_barrier_semaphore()

    def greet(i, carry):
        peers(
            lax.rem(CHUNKS + 2 - i, CHUNKS),
            1,
            lambda n, device: pl.semaphore_signal(
                barrier, inc=1, device_id=device, device_id_type=MESH
            ),
        )
        return carry

    lax.fori_loop(0, CHUNKS, greet, 0)
    small = [
        pltpu.make_async_copy(src, dst, in_sem.at[i])
        for i, (src, dst) in enumerate(
            ((routes_hbm, routes), (sub_hbm, sub), (tokens_hbm, tokens))
        )
    ]
    loads = []
    for e in range(win.shape[0]):
        loads.append(pltpu.make_async_copy(win_hbm.at[e], win.at[e], w_sem.at[2 * e]))
        loads.append(pltpu.make_async_copy(
            wout_hbm.at[e], wout.at[pl.ds(e * units, units)], w_sem.at[2 * e + 1]
        ))
    for load in small:
        load.start()
    for load in small:
        load.wait()
    for load in loads:
        load.start()

    owner = routes[...]
    dz = ((owner >> 5) + (NZ - z)) & (NZ - 1)
    dy = ((owner >> 3) + (NY - y)) & (NY - 1)
    dx = ((owner >> 1) + (NX - x)) & (NX - 1)
    dc = (owner + (NC - c)) & (NC - 1)
    chip = dz * (NY * NX) + dy * NX + dx
    rank = jnp.zeros_like(chip)
    for i, (a, b, d) in enumerate(ORDER):
        rank = jnp.where(chip == a * (NY * NX) + b * NX + d, i, rank)
    number = rank * NC + dc
    row, lane = iota((n_tok, n_tok), 0), iota((n_tok, n_tok), 1)
    diagonal = row == lane
    number_row = number.astype(F32)
    sub_row = sub[...].astype(F32)
    number_col = jnp.sum(jnp.where(diagonal, number_row, 0.0), axis=1, keepdims=True)
    sub_col = jnp.sum(jnp.where(diagonal, sub_row, 0.0), axis=1, keepdims=True)
    same = jnp.where(number_col == number_row, 1.0, 0.0)
    slot_row = jnp.sum(jnp.where(row < lane, same, 0.0), axis=0, keepdims=True)
    slot_col = jnp.sum(jnp.where(lane < row, same, 0.0), axis=1, keepdims=True)
    target_row = (number_row * (2 * CAP) + slot_row).astype(jnp.int32)
    target_col = (number_col * (2 * CAP) + slot_col).astype(jnp.int32)

    peer = iota((CHUNKS * PER, n_tok), 0).astype(F32)
    lanes = iota((n_tok, 128), 1).astype(F32)
    chosen = jnp.where(slot_col == lanes, sub_col, 0.0).astype(BF)
    labels[...] = (
        jnp.dot(onehot(peer == number_row), chosen, preferred_element_type=F32)
        .astype(jnp.int32)
        .reshape(labels.shape)
    )

    rows = PER * 2 * CAP
    place_row = iota((rows, n_tok), 0)

    def place(k, carry):
        at = place_row + k * rows
        block = jnp.dot(
            onehot(at == target_row), tokens[:, :half], preferred_element_type=F32
        )
        block += jnp.dot(
            onehot(at == target_row + CAP), tokens[:, half:], preferred_element_type=F32
        )
        send[pl.ds(k * PER, PER)] = block.astype(BF).reshape(PER, 2 * CAP, half)
        return carry

    lax.fori_loop(0, CHUNKS, place, 0)

    pl.semaphore_wait(barrier, CHUNKS * PER - 1)

    pltpu.make_async_copy(labels.at[0], labels_in.at[0], lrecv_sem.at[0]).start()
    pltpu.make_async_copy(send.at[0], recv.at[0], recv_sem.at[0]).start()

    def dispatch(k, carry):
        def visit(n, device):
            push(labels.at[n], labels_in.at[n], lsend_sem, lrecv_sem.at[k], device)
            push(send.at[n], recv.at[n], send_sem, recv_sem.at[k], device)

        peers(k, 1, visit)
        return carry

    lax.fori_loop(0, CHUNKS, dispatch, 0)

    m = PER * CAP
    to, fro = iota((rows, rows), 0), iota((rows, rows), 1)

    def origin(r):
        return ((r & (m - 1)) >> 2) * (2 * CAP) + (r >> 7) * CAP + (r & (CAP - 1))

    split = onehot(fro == origin(to))
    join = onehot(to == origin(fro))
    spread = onehot((iota((m, PER), 0) >> 2) == iota((m, PER), 1))
    own_lane = (iota((m, 128), 0) & (CAP - 1)) == iota((m, 128), 1)

    for load in loads:
        load.wait()

    def compute(k, carry):
        mine = pl.ds(k * PER, PER)
        pltpu.make_async_copy(labels.at[mine], labels_in.at[mine], lrecv_sem.at[k]).wait()
        label = jnp.dot(
            spread,
            labels_in[mine].reshape(PER, 128).astype(F32).astype(BF),
            preferred_element_type=F32,
        )
        label = jnp.sum(jnp.where(own_lane, label, 0.0), axis=1, keepdims=True)
        pltpu.make_async_copy(send.at[mine], recv.at[mine], recv_sem.at[k]).wait()
        arrived = recv[mine].reshape(rows, half)
        halves = jnp.dot(split, arrived, preferred_element_type=F32)
        batch = jnp.concatenate([halves[:m], halves[m:]], axis=1)
        for e in range(win.shape[0]):
            part = jnp.where(label == e, batch, 0.0).astype(BF)
            hidden[:, e * units : (e + 1) * units] = jnp.maximum(
                jnp.dot(part, win[e], preferred_element_type=F32), 0.0
            ).astype(BF)
        total = jnp.dot(hidden[...], wout[...], preferred_element_type=F32)
        total = total.astype(BF)
        stacked = jnp.concatenate([total[:, :half], total[:, half:]], axis=0)
        block = jnp.dot(join, stacked, preferred_element_type=F32).astype(BF)
        back[mine] = block.reshape(PER, 2 * CAP, half)

        @pl.when(k == 0)
        def _():
            pltpu.make_async_copy(back.at[0], home.at[0], home_sem.at[0]).start()

        peers(
            k,
            -1,
            lambda n, device: push(back.at[n], home.at[n], bsend_sem, home_sem.at[k], device),
        )
        return carry

    lax.fori_loop(0, CHUNKS, compute, 0)

    take_lane = iota((n_tok, rows), 1)
    out_left = out_right = None
    for k in (0, 1, 3, 2):
        mine = pl.ds(k * PER, PER)
        at = take_lane + k * rows
        take_left = onehot(at == target_col)
        take_right = onehot(at == target_col + CAP)
        pltpu.make_async_copy(back.at[mine], home.at[mine], home_sem.at[k]).wait()
        returned = home[mine].reshape(rows, half)
        a = jnp.dot(take_left, returned, preferred_element_type=F32)
        b = jnp.dot(take_right, returned, preferred_element_type=F32)
        out_left = a if k == 0 else out_left + a
        out_right = b if k == 0 else out_right + b
    out[:, :half] = out_left.astype(BF)
    out[:, half:] = out_right.astype(BF)

    others = pl.ds(1, CHUNKS * PER - 1)
    pltpu.make_async_copy(labels.at[others], labels_in.at[others], lsend_sem).wait()
    pltpu.make_async_copy(send.at[others], recv.at[others], send_sem).wait()
    pltpu.make_async_copy(back.at[others], home.at[others], bsend_sem).wait()


def pinned(operand):
    return pltpu.with_memory_space_constraint(operand, pltpu.MemorySpace.HBM)


def local(tokens, routes, sub_expert, probability, weight_in, weight_out):
    n_tok, width = tokens.shape
    experts, _, units = weight_in.shape
    n = CHUNKS * PER
    blocks = pltpu.VMEM((n, 2 * CAP, width // 2), BF)
    dma = pltpu.SemaphoreType.DMA
    gathered = pl.pallas_call(
        kernel,
        out_shape=jax.ShapeDtypeStruct((n_tok, width), BF),
        in_specs=[pl.BlockSpec(memory_space=pltpu.MemorySpace.HBM)] * 5,
        out_specs=pl.BlockSpec(memory_space=pltpu.VMEM),
        scratch_shapes=[
            pltpu.VMEM((n_tok, width), BF),
            pltpu.VMEM((1, n_tok), jnp.int32),
            pltpu.VMEM((1, n_tok), jnp.int32),
            pltpu.VMEM(weight_in.shape, BF),
            pltpu.VMEM((experts * units, width), BF),
            blocks, blocks, blocks, blocks,
            pltpu.VMEM((n, 1, 128), jnp.int32),
            pltpu.VMEM((n, 1, 128), jnp.int32),
            pltpu.VMEM((PER * CAP, experts * units), BF),
            dma((3,)), dma((2 * experts,)),
            dma, dma((CHUNKS,)), dma, dma((CHUNKS,)), dma, dma((CHUNKS,)),
        ],
        compiler_params=pltpu.CompilerParams(
            collective_id=0, has_side_effects=True, vmem_limit_bytes=56000000
        ),
    )(
        tokens,
        pinned(routes.reshape(1, n_tok)),
        pinned(sub_expert.reshape(1, n_tok)),
        weight_in,
        weight_out,
    )
    return (gathered.astype(F32) * probability[:, None]).astype(BF)


def solution(mesh):
    return jax.shard_map(
        local,
        mesh=mesh,
        in_specs=(
            P(("ex", "ey"), None),
            P(("ex", "ey"), None),
            P(("ex", "ey")),
            P(("ex", "ey")),
            P(("ex", "ey"), None, None),
            P(("ex", "ey"), None, None),
        ),
        out_specs=P(("ex", "ey"), None),
        check_vma=False,
    )
```
